32 devices in a mesh: blk: 8 (over y, x, core), grp: 4 (over z).
Axes of the slice: x: 2, y: 2, z: 4, core: 2. Of those that a mesh axis runs over, the one named last changes fastest.
Arguments:
- node_feats: bfloat16 [8192, 512], P(('blk', 'grp')), may hold values from -6 to 6
- w_local: bfloat16 [512, 512], replicated, may hold values from -0.25 to 0.25
- w_gate: bfloat16 [512, 512], replicated, may hold values from -0.25 to 0.25
- w_query: bfloat16 [512, 512], replicated, may hold values from -0.25 to 0.25
- w_key: bfloat16 [512, 512], replicated, may hold values from -0.25 to 0.25
- w_value: bfloat16 [512, 512], replicated, may hold values from -0.25 to 0.25
- norm_gain: float32 [512], replicated, may hold values from 0.1 to 1.9
- tile_weights: int32 [8, 8, 4, 8, 128, 128], P('blk', None, 'grp'), may hold values from 0 to 2
- tile_slots: int32 [8, 8, 4, 8], P('blk', None, 'grp'), may hold values from 0 to 15, as said below
- tile_counts: int32 [8, 8, 4], P('blk', None, 'grp'), may hold values from 1 to 8, as said below
Outputs:
- layer_out: bfloat16 [8192, 512], P(('blk', 'grp'))
The draws below stay inside these ranges and needn't reach their ends.
Inputs may be any that keep to these rules, and one draw needn't show every extreme that they name: `tile_counts`: some block pair has all 8 slots live in every draw. `tile_slots`: the 8 slots of one block pair name different tile positions.
All inputs are finite; a program needn't handle non-finite values.
Results may differ from the reference program's by a relative error of at most 0.0085.
Values may be sent and summed in bfloat16 or wider, within the bound.
No kernel may reach another device: no remote copies, remote signals or barrier semaphores. Data moves between devices by JAX's collectives and lax.ppermute only.
A program may use at most 128 MiB of HBM per device.

```python
import jax
import jax.numpy as jnp
from jax import lax

D = 512
HEADS = 8
ROWS_DEV = 256
TILE = 128
MAXT = 8
HOPS = 2
NODES = 8192
N_BLK = 8
N_GRP = 4


def draw_tile_counts(key, part):
    key = jax.random.fold_in(key, 101)
    key_block, key_group, key_diag, key_near, key_far = jax.random.split(key, 5)
    busy_block = jax.random.randint(key_block, (), 0, N_BLK)
    busy_group = jax.random.randint(key_group, (), 0, N_GRP)
    block_ids = jnp.arange(N_BLK, dtype=jnp.int32)
    shape = (N_BLK, N_BLK, N_GRP)
    ahead = jnp.mod(block_ids[None, :] - block_ids[:, None], N_BLK)
    behind = jnp.mod(block_ids[:, None] - block_ids[None, :], N_BLK)
    distance = jnp.minimum(ahead, behind)[:, :, None]
    half_most = max(MAXT // 2, 1)
    dense = jax.random.randint(key_diag, shape, half_most, MAXT + 1)
    near = jax.random.randint(key_near, shape, half_most, MAXT + 1)
    far = jnp.minimum(jax.random.randint(key_far, shape, half_most // 2 + 1, half_most + 2), MAXT)
    is_busy = block_ids[:, None, None] == busy_block
    counts = jnp.where(distance == 0, dense, jnp.where(distance == 1, near, far))
    counts = jnp.where(is_busy & (distance >= 1) & (distance <= 2), dense, counts)
    forced = is_busy & (distance == 0) & (jnp.arange(N_GRP, dtype=jnp.int32)[None, None, :] == busy_group)
    return jnp.where(forced, MAXT, counts).astype(jnp.int32)


def draw_tile_slots(key, part):
    key = jax.random.fold_in(key, 202)
    positions = N_GRP * (ROWS_DEV // TILE) * (ROWS_DEV // TILE)
    scores = jax.random.randint(key, (N_BLK, N_BLK, N_GRP, positions), 0, 1 << 16) * positions + jnp.arange(positions, dtype=jnp.int32)
    order = jnp.argsort(scores, axis=-1)
    return order[..., :MAXT].astype(jnp.int32)


def draw_tile_weights(key, part):
    key = jax.random.fold_in(key, 303)
    key_edge, key_value = jax.random.split(key, 2)
    shape = (N_BLK, N_BLK, N_GRP, MAXT, TILE, TILE)
    edges = jax.random.randint(key_edge, shape, 0, 16) == 0
    values = jax.random.randint(key_value, shape, 1, 3)
    return jnp.where(edges, values, 0).astype(jnp.int32)


def levels(stream_key, extent, cuts, smallest, high):
    level, own = 1.0, jax.random.fold_in(stream_key, 6)
    for axis_at, shards_of in cuts:
        heights = jnp.exp(jax.random.uniform(jax.random.fold_in(own, axis_at), (shards_of,), jnp.float32, smallest / len(cuts), high / len(cuts)))
        level = level * jnp.repeat(heights, extent[axis_at] // shards_of).reshape([-1 if axis == axis_at else 1 for axis in range(len(extent))])
    return level


def normal_values(stream_key, dims, width, bound, pieces=(), kind=jnp.bfloat16):
    gain = levels(stream_key, dims, pieces, -0.22, 0.18) if pieces else 1.0
    array = jax.random.normal(stream_key, dims, jnp.float32) * width * gain
    return jnp.minimum(jnp.maximum(array, -bound), bound).astype(kind)


def setup_inputs(seed: int = 0) -> dict:
    arg_keys = jax.random.split(jax.random.key(seed), 11)
    node_feats = normal_values(arg_keys[0], (NODES, D), 1.0, 6.0, ((0, 32),))
    w_local = normal_values(arg_keys[1], (D, D), D ** -0.5, 0.25)
    w_gate = normal_values(arg_keys[2], (D, D), D ** -0.5, 0.25)
    w_query = normal_values(arg_keys[3], (D, D), D ** -0.5, 0.25)
    w_key = normal_values(arg_keys[4], (D, D), D ** -0.5, 0.25)
    w_value = normal_values(arg_keys[5], (D, D), D ** -0.5, 0.25)
    norm_gain = jnp.clip(1.0 + 0.18 * jax.random.normal(arg_keys[6], (D,), jnp.float32), 0.1, 1.9)
    tile_weights = draw_tile_weights(jax.random.fold_in(arg_keys[10], 71), 0)
    tile_slots = draw_tile_slots(jax.random.fold_in(arg_keys[10], 71), 0)
    tile_counts = draw_tile_counts(jax.random.fold_in(arg_keys[10], 71), 0)
    return {"node_feats": node_feats, "w_local": w_local, "w_gate": w_gate, "w_query": w_query, "w_key": w_key, "w_value": w_value, "norm_gain": norm_gain, "tile_weights": tile_weights, "tile_slots": tile_slots, "tile_counts": tile_counts}


norm_eps = 1e-05

def reference(node_feats, w_local, w_gate, w_query, w_key, w_value, norm_gain, tile_weights, tile_slots, tile_counts):
    col_tiles = ROWS_DEV // TILE
    row_tiles = N_GRP * col_tiles
    block_rows = N_GRP * ROWS_DEV
    live_slots = jnp.arange(MAXT, dtype=jnp.int32)[None, None, None, :] < tile_counts[..., None]
    rows_of = (tile_slots // col_tiles).astype(jnp.int32)
    cols_of = (tile_slots % col_tiles).astype(jnp.int32)
    base_tiles = (jnp.arange(N_BLK, dtype=jnp.int32)[:, None, None] * N_GRP + jnp.arange(N_GRP, dtype=jnp.int32)[None, :, None]) * col_tiles
    source_ids = (base_tiles[None] + cols_of).astype(jnp.int32)

    def propagate(feats):
        feat_tiles = feats.astype(jnp.float32).reshape(NODES // TILE, TILE, D)

        def one_block(inputs):
            block_wts, block_live, block_rows_of, block_src = inputs
            masked = jnp.where(block_live[..., None, None], block_wts, 0).astype(jnp.float32)
            row_pick = (block_rows_of[..., None] == jnp.arange(row_tiles, dtype=jnp.int32)).astype(jnp.float32)
            sources = feat_tiles[block_src]
            product = jnp.einsum('jgtil,jgtld->jgtid', masked, sources, precision=lax.Precision.HIGHEST)
            summed = jnp.einsum('jgtr,jgtid->rid', row_pick, product, precision=lax.Precision.HIGHEST)
            degree = jnp.einsum('jgtr,jgti->ri', row_pick, lax.optimization_barrier(jnp.sum(masked, axis=-1)), precision=lax.Precision.HIGHEST)
            return (summed.reshape(block_rows, D), degree.reshape(block_rows))
        summed, degree = lax.map(one_block, (tile_weights, live_slots, rows_of, source_ids))
        return (summed.reshape(NODES, D), degree.reshape(NODES))
    feats = jnp.dot(node_feats, w_local, preferred_element_type=jnp.float32).astype(jnp.bfloat16)
    for hop_index in range(HOPS):
        summed, degree = propagate(feats)
        scale = lax.rsqrt(degree + 1.0)
        feats = ((summed + feats.astype(jnp.float32)) * scale[:, None]).astype(jnp.bfloat16)
    gate = jnp.dot(node_feats, w_gate, preferred_element_type=jnp.float32)
    queries = jax.nn.sigmoid(jnp.dot(node_feats, w_query, preferred_element_type=jnp.float32)).astype(jnp.bfloat16)
    keys_all = jax.nn.sigmoid(jnp.dot(node_feats, w_key, preferred_element_type=jnp.float32)).astype(jnp.bfloat16)
    values_all = jnp.dot(node_feats, w_value, preferred_element_type=jnp.float32).astype(jnp.bfloat16)
    head_size = D // HEADS
    queries = queries.astype(jnp.float32).reshape(NODES, HEADS, head_size)
    keys_all = keys_all.astype(jnp.float32).reshape(NODES, HEADS, head_size)
    values_all = values_all.astype(jnp.float32).reshape(NODES, HEADS, head_size)
    summary = jnp.einsum('nhd,nhe->hde', keys_all, values_all, precision=lax.Precision.HIGHEST)
    summary_b = summary.astype(jnp.bfloat16).astype(jnp.float32)
    attended = jnp.einsum('nhd,hde->nhe', queries, summary_b, precision=lax.Precision.HIGHEST).reshape(NODES, D)
    mean_val = lax.optimization_barrier(jnp.mean(attended, axis=1, keepdims=True))
    centered = attended - mean_val
    var_val = lax.optimization_barrier(jnp.mean(centered * centered, axis=1, keepdims=True))
    glob = centered * lax.rsqrt(var_val + norm_eps) * norm_gain[None, :]
    total = node_feats.astype(jnp.float32) + feats.astype(jnp.float32) * gate + glob
    return total.astype(jnp.bfloat16)
```

```python
import jax
import jax.numpy as jnp
from jax import lax
from jax.experimental import pallas as pl
from jax.experimental.pallas import tpu as pltpu
from jax.sharding import PartitionSpec as P

HEADS = 8
HOPS = 2
CHUNKS = 2


norm_eps = 1e-05


def swap(value, axis, mask):
    size = lax.axis_size(axis)
    return lax.ppermute(value, axis, [(i, i ^ mask) for i in range(size)])


def prepare(weights, slots, counts, my_block, row_tiles, col_tiles):
    blocks, slot_most, tile, _ = weights.shape
    rows, cols = row_tiles * tile, col_tiles * tile

    def kernel(me_ref, slots_ref, counts_ref, w_ref, a_ref, deg_ref, acc_ref):
        step = pl.program_id(0)
        source = me_ref[0] ^ step
        a_ref[...] = jnp.zeros_like(a_ref)

        @pl.when(step == 0)
        def _():
            acc_ref[...] = jnp.zeros_like(acc_ref)

        for slot in range(slot_most):

            @pl.when(slot < counts_ref[source])
            def _():
                place = slots_ref[source, slot]
                row = pl.multiple_of((place // col_tiles) * tile, tile)
                col = pl.multiple_of((place % col_tiles) * tile, tile)
                values = w_ref[0, slot].astype(jnp.float32)
                a_ref[pl.ds(row, tile), pl.ds(col, tile)] = values.astype(jnp.bfloat16)
                acc_ref[pl.ds(row, tile), :] += values

        @pl.when(step == blocks - 1)
        def _():
            ones = jnp.ones((8, tile), jnp.bfloat16)
            total = acc_ref[...].astype(jnp.bfloat16)
            deg_ref[...] = lax.dot_general(
                ones, total, (((1,), (1,)), ((), ())), preferred_element_type=jnp.float32
            )

    return pl.pallas_call(
        kernel,
        out_shape=(
            jax.ShapeDtypeStruct((rows, blocks * cols), jnp.bfloat16),
            jax.ShapeDtypeStruct((8, rows), jnp.float32),
        ),
        grid_spec=pltpu.PrefetchScalarGridSpec(
            num_scalar_prefetch=3,
            grid=(blocks,),
            in_specs=[
                pl.BlockSpec(
                    (1, slot_most, tile, tile), lambda s, me, sl, ct: (me[0] ^ s, 0, 0, 0)
                )
            ],
            out_specs=(
                pl.BlockSpec((rows, cols), lambda s, me, sl, ct: (0, s)),
                pl.BlockSpec((8, rows), lambda s, me, sl, ct: (0, 0)),
            ),
            scratch_shapes=[pltpu.VMEM((rows, tile), jnp.float32)],
        ),
        compiler_params=pltpu.CompilerParams(vmem_limit_bytes=16 << 20),
        cost_estimate=pl.CostEstimate(
            flops=rows * blocks * cols, bytes_accessed=weights.size * 4 + rows * blocks * cols * 2, transcendentals=0
        ),
        name="prepare",
    )(my_block, slots, counts, weights)


def local(
    node_feats,
    w_local,
    w_gate,
    w_query,
    w_key,
    w_value,
    norm_gain,
    tile_weights,
    tile_slots,
    tile_counts,
):
    row_count, feat_width = node_feats.shape
    tile_size = tile_weights.shape[-1]
    blocks = lax.axis_size("blk")
    groups = lax.axis_size("grp")
    col_tiles = row_count // tile_size
    row_tiles = groups * col_tiles
    my_block = lax.axis_index("blk")
    my_group = lax.axis_index("grp")
    width = feat_width // CHUNKS

    adjacency, degree_part = prepare(
        tile_weights[0, :, 0],
        tile_slots[0, :, 0],
        tile_counts[0, :, 0],
        my_block.astype(jnp.int32)[None],
        row_tiles,
        col_tiles,
    )
    degree = degree_part[0]
    step = 1
    while step < groups:
        degree = degree + swap(degree, "grp", step)
        step *= 2
    degree_rows = lax.dynamic_slice_in_dim(degree, my_group * row_count, row_count)
    scale = lax.rsqrt(degree_rows + 1.0)[:, None]

    def one_hop(feats):
        pieces = [feats] + [swap(feats, "blk", m) for m in range(2, blocks, 2)]
        mine = jnp.concatenate(pieces)
        other = swap(mine, "blk", 1)
        gathered = jnp.stack([mine.reshape(blocks // 2, row_count, -1), other.reshape(blocks // 2, row_count, -1)], axis=1)
        partial = jnp.dot(adjacency, gathered.reshape(blocks * row_count, -1), preferred_element_type=jnp.float32)
        partial = partial.reshape(groups, row_count, -1)

        def chunk(mask):
            return lax.dynamic_index_in_dim(partial, my_group ^ mask, 0, keepdims=False)

        total = chunk(0) + feats.astype(jnp.float32)
        for m in range(groups - 1, 0, -1):
            total = total + swap(chunk(m).astype(jnp.bfloat16), "grp", m).astype(jnp.float32)
        return (total * scale).astype(jnp.bfloat16)

    feats = jnp.dot(node_feats, w_local, preferred_element_type=jnp.float32).astype(jnp.bfloat16)
    columns = [feats[:, i * width : (i + 1) * width] for i in range(CHUNKS)]
    for hop_index in range(HOPS):
        columns = [one_hop(column) for column in columns]
    head_size = feat_width // HEADS
    queries = jax.nn.sigmoid(
        jnp.dot(node_feats, w_query, preferred_element_type=jnp.float32)
    ).astype(jnp.bfloat16)
    keys_here = jax.nn.sigmoid(
        jnp.dot(node_feats, w_key, preferred_element_type=jnp.float32)
    ).astype(jnp.bfloat16)
    values_here = jnp.dot(node_feats, w_value, preferred_element_type=jnp.float32).astype(
        jnp.bfloat16
    )
    queries = queries.reshape(row_count, HEADS, head_size)
    keys_here = keys_here.reshape(row_count, HEADS, head_size)
    values_here = values_here.reshape(row_count, HEADS, head_size)
    summary = jnp.einsum(
        "nhd,nhe->hde", keys_here, values_here, preferred_element_type=jnp.float32
    )
    summary = summary.reshape(-1, 128)
    for axis, size in (("blk", blocks), ("grp", groups)):
        step = 1
        while step < size:
            summary = summary + swap(summary, axis, step)
            step *= 2
    summary_b = summary.astype(jnp.bfloat16).reshape(HEADS, head_size, head_size)
    attended = jnp.einsum(
        "nhd,hde->nhe", queries, summary_b, preferred_element_type=jnp.float32
    ).reshape(row_count, feat_width)
    mean_val = jnp.mean(attended, axis=1, keepdims=True)
    centered = attended - mean_val
    var_val = jnp.mean(centered * centered, axis=1, keepdims=True)
    glob = centered * lax.rsqrt(var_val + norm_eps) * norm_gain[None, :]
    gate = jnp.dot(node_feats, w_gate, preferred_element_type=jnp.float32)
    base = node_feats.astype(jnp.float32) + glob
    total = base + jnp.concatenate(columns, axis=1).astype(jnp.float32) * gate
    return total.astype(jnp.bfloat16)


def solution(mesh):
    in_specs = (
        P(("blk", "grp"), None),
        P(),
        P(),
        P(),
        P(),
        P(),
        P(),
        P("blk", None, "grp", None, None, None),
        P("blk", None, "grp", None),
        P("blk", None, "grp"),
    )
    out_specs = P(("blk", "grp"), None)
    return jax.shard_map(local, mesh=mesh, in_specs=in_specs, out_specs=out_specs, check_vma=False)
```
